32 devices in a mesh: groups: 2 (over x), modes: 16 (over z, y, core).
Axes of the slice: x: 2, y: 2, z: 4, core: 2. Of those that a mesh axis runs over, the one named last changes fastest.
Arguments:
- mode_fields: bfloat16 [256, 256, 2048], P(('groups', 'modes')), parts along dimension 0, may hold values from -0.59765625 to 0.59765625
- coeff: float32 [256], P('groups'), parts along dimension 0, may hold values from -6 to 6
- eigen: float32 [256], P('groups'), parts along dimension 0, may hold values from 0.1 to 100
- map_friction: float32 [512, 2048], P(('groups', 'modes')), parts along dimension 0, may hold values from 1 to 2.5
- bed: float32 [512, 2048], P(('groups', 'modes')), parts along dimension 0, may hold values from -5 to 5
- smb: float32 [512, 2048], P(('groups', 'modes')), parts along dimension 0, may hold values from -0.6 to 0.4
- thickness: float32 [512, 2048], P(('groups', 'modes')), parts along dimension 0, may hold values from 1.9 to 2.6
Outputs:
- log_friction: float32 [512, 2048], P(('groups', 'modes')), parts along dimension 0
- final_thickness: float32 [512, 2048], P(('groups', 'modes')), parts along dimension 0
The draws below stay inside these ranges and needn't reach their ends.
There are 2 independent parts, one for each index of `groups`. The reference program is written for one: setup_inputs(seed, part) draws one part's arguments, and reference() takes and returns one part's arrays. A program takes and returns all parts, laid end to end along the dimension named above; each array names one. Nothing has to cross between parts.
All inputs are finite; a program needn't handle non-finite values.
Results may differ from the reference program's by a relative error of at most 0.0014.
Values may be sent and summed in bfloat16 or wider, within the bound.
A program may use at most 64 MiB of HBM per device.

```python
import math
import jax
import jax.numpy as jnp

MODES = 128
NY = 2048
STEPS = 8
NX = 256


def draw_bed(key, part):
    key_list = jax.random.split(jax.random.fold_in(key, 17), 2)
    phase_pair = jax.random.uniform(key_list[0], (2,), jnp.float32, 0.0, 2.0 * math.pi)
    row_index = jnp.arange(NX, dtype=jnp.float32)[:, None]
    column_index = jnp.arange(NY, dtype=jnp.float32)[None, :]
    wave_number = 2.0 * math.pi / 48.0
    amplitude = 2.0
    roughness = jnp.clip(0.25 * jax.random.normal(key_list[1], (NX, NY), jnp.float32), -0.75, 0.75)
    smooth_part = amplitude * (jnp.sin(wave_number * row_index + phase_pair[0]) + jnp.sin(wave_number * column_index + phase_pair[1]))
    return (smooth_part + roughness).astype(jnp.float32)


def with_spikes(drawn, stream_key, source, target, parts, factor):
    owner, partner = [(jnp.arange(drawn.shape[axis_at]) // (drawn.shape[axis_at] // parts)).reshape([-1 if axis == axis_at else 1 for axis in range(drawn.ndim)]) for axis_at in (source, target)]
    chosen = jax.random.permutation(stream_key, parts)[partner]
    strong = (owner == chosen) | (owner == (partner + parts // 2) % parts)
    return jnp.where(strong, factor * drawn, drawn)


def block_scale(own_key, extent, cuts, smallest, largest):
    level, own = 1.0, jax.random.fold_in(own_key, 6)
    for position, parts in cuts:
        heights = jnp.exp(jax.random.uniform(jax.random.fold_in(own, position), (parts,), jnp.float32, smallest / len(cuts), largest / len(cuts)))
        level = level * jnp.repeat(heights, extent[position] // parts).reshape([-1 if axis == position else 1 for axis in range(len(extent))])
    return level


def centred(stream_key, extent, width, most, cuts=(), kind=jnp.bfloat16):
    gain = block_scale(stream_key, extent, cuts, -0.22, 0.18) if cuts else 1.0
    drawn = jax.random.normal(stream_key, extent, jnp.float32) * width * gain
    return jnp.minimum(jnp.maximum(drawn, -most), most).astype(kind)


def bell_draw_with(stream_key, dims, deviation, reach, cuts, heavy, kind=jnp.bfloat16):
    drawn = deviation * jax.random.normal(stream_key, dims, jnp.float32)
    if cuts:
        drawn = drawn * block_scale(stream_key, dims, cuts, -0.22, 0.18)
    return jnp.clip(with_spikes(drawn, jax.random.fold_in(stream_key, 3), *heavy), -reach, reach).astype(kind)


def setup_inputs(seed: int = 0, part: int = 0) -> dict:
    streams_of = jax.random.split(jax.random.key(seed), 8)
    part_splits = jax.random.split(jax.random.fold_in(streams_of[7], part), 8)
    return {
        "mode_fields": bell_draw_with(part_splits[0], (MODES, NX, NY), 0.1, 0.59765625, ((0, 16),), (0, 1, 16, 2.0)),
        "coeff": centred(part_splits[1], (MODES,), 1.0, 6.0, (), jnp.float32),
        "eigen": jnp.clip(jnp.exp(jax.random.uniform(part_splits[2], (MODES,), jnp.float32, math.log(0.1), math.log(100.0))), 0.1, 100.0),
        "map_friction": jnp.clip(1.0 + 1.5 * jax.random.uniform(part_splits[3], (NX, NY), jnp.float32) ** block_scale(part_splits[3], (NX, NY), ((0, 16),), -0.2, 0.2), 1.0, 2.5),
        "bed": draw_bed(jax.random.fold_in(jax.random.fold_in(streams_of[7], part), 71), part),
        "smb": jnp.clip(-0.6 + 1 * jax.random.uniform(part_splits[5], (NX, NY), jnp.float32) ** block_scale(part_splits[5], (NX, NY), ((0, 16),), -0.2, 0.2), -0.6, 0.4),
        "thickness": jnp.clip(1.9 + 0.6999999 * jax.random.uniform(part_splits[6], (NX, NY), jnp.float32) ** block_scale(part_splits[6], (NX, NY), ((0, 16),), -0.2, 0.2), 1.9, 2.6),
    }


flow_rate = 0.02
slide_rate = 0.1
diff_cap = 0.5
time_step = 0.4

def advance(height, base, friction, balance):
    hpad = jnp.pad(height, ((0, 0), (2, 2)))
    bpad = jnp.pad(base, ((0, 0), (2, 2)))
    fpad = jnp.pad(friction, ((0, 0), (2, 2)))
    surface = bpad + hpad
    grad_x = (surface[2:, 1:-1] - surface[:-2, 1:-1]) * 0.5
    grad_y = (surface[1:-1, 2:] - surface[1:-1, :-2]) * 0.5
    center = hpad[1:-1, 1:-1]
    fcent = fpad[1:-1, 1:-1]
    squared = center * center
    diff = flow_rate * squared * squared * center * (grad_x * grad_x + grad_y * grad_y)
    diff = jnp.minimum(diff + slide_rate * squared * jnp.exp(-fcent), diff_cap)
    scent = surface[1:-1, 1:-1]
    mid_d = diff[1:-1, 1:-1]
    mid_s = scent[1:-1, 1:-1]
    up_x = 0.5 * (diff[2:, 1:-1] + mid_d) * (scent[2:, 1:-1] - mid_s)
    down_x = 0.5 * (mid_d + diff[:-2, 1:-1]) * (mid_s - scent[:-2, 1:-1])
    up_y = 0.5 * (diff[1:-1, 2:] + mid_d) * (scent[1:-1, 2:] - mid_s)
    down_y = 0.5 * (mid_d + diff[1:-1, :-2]) * (mid_s - scent[1:-1, :-2])
    total = up_x - down_x + up_y - down_y
    return jnp.maximum(height[2:-2] + time_step * (total + balance[2:-2]), 0.0)

def reference(mode_fields, coeff, eigen, map_friction, bed, smb, thickness):
    weights = (coeff / jnp.sqrt(1.0 + eigen)).astype(jnp.bfloat16)
    flat = mode_fields.reshape(MODES, NX * NY)
    perturb = jnp.dot(weights[None, :], flat, preferred_element_type=jnp.float32).reshape(NX, NY)
    log_friction = map_friction + perturb
    rim = ((2, 2), (0, 0))
    base = jnp.pad(bed, rim)
    friction = jnp.pad(log_friction, rim)
    balance = jnp.pad(smb, rim)
    height = thickness
    for step in range(STEPS):
        height = advance(jnp.pad(height, rim), base, friction, balance)
    return (log_friction, height)
```

```python
import functools

import jax
import jax.numpy as jnp
from jax import lax
from jax.experimental import pallas as pl
from jax.experimental.pallas import tpu as pltpu
from jax.sharding import PartitionSpec as P

STEPS = 8

flow_rate = 0.02
slide_rate = 0.1
diff_cap = 0.5
time_step = 0.4

WIRE = jnp.bfloat16
PAD = 8
LANES = 128
GROUP = 4
F32 = jnp.float32


def flip(x, k):
    bit = 1
    while bit <= k:
        if k & bit:
            x = x + bit - 2 * bit * (x // bit % 2)
        bit *= 2
    return x


def gather_kernel(
    n, H,
    coeff_hbm, eigen_hbm, map_hbm, bed_hbm, smb_hbm, h0_hbm, fields_ref,
    logf_ref, ext_b, ext_e, ext_m, ext_h, ext_s,
    coeff_ref, eigen_ref, map_ref, bed_ref, smb_ref, h0_ref, in_sem,
    mf, p1out, p1own, p1in, s2out, s2in, s3out, s3in,
    st_out, st_in, f_out, f_in,
    mf_sem, p1s, p1r, s2s, s2r, s3s, s3r, hs, hr,
):
    me = lax.axis_index("modes")
    c = me % 2
    a = (me // 2) % 2
    b = me // 4
    B = n // 4
    mode_dev = fields_ref.shape[0]
    rows, cols = map_ref.shape
    cw = cols // H
    ks = list(range(B - 1, -1, -1))
    Q = B * H

    hbm = (coeff_hbm, eigen_hbm, bed_hbm, smb_hbm, h0_hbm, map_hbm)
    own = (coeff_ref, eigen_ref, bed_ref, smb_ref, h0_ref, map_ref)
    takes = [pltpu.make_async_copy(x, y, in_sem.at[i]) for i, (x, y) in enumerate(zip(hbm, own))]
    for take in takes:
        take.start()

    def load(i):
        k, aa, hh, cc = B - 1 - i // (2 * H) % B, 1 - i // (2 * Q), i // 2 % H, 1 - i % 2
        bit, z = 1, b
        while bit < B:
            on = k // bit % 2
            z = z + on * (bit - 2 * bit * (b // bit % 2))
            bit *= 2
        strip = (z * 2 + (a + aa - 2 * a * aa)) * 2 + (c + cc - 2 * c * cc)
        rr = pl.ds(pl.multiple_of(strip * rows, rows), rows)
        cc_ = pl.ds(pl.multiple_of(hh * cw, cw), cw)
        return pltpu.make_async_copy(fields_ref.at[:, rr, cc_], mf.at[i], mf_sem.at[i])

    def go(i, carry):
        load(i).start()
        return carry
    lax.fori_loop(0, n * H, go, 0)

    left, right = lax.rem(me + n - 1, n), lax.rem(me + 1, n)
    core_peer = me + 1 - 2 * c
    y_peer = me + 2 - 4 * a
    barrier = pltpu.get_barrier_semaphore()

    def z_peer(k):
        return (flip(b, k) * 2 + a) * 2 + c

    for peer in [left, right, core_peer, y_peer] + [z_peer(k) for k in range(1, B)]:
        pl.semaphore_signal(barrier, inc=1, device_id={"modes": peer}, device_id_type=pl.DeviceIdType.MESH)

    takes[0].wait()
    takes[1].wait()
    w = coeff_ref[...] / jnp.sqrt(1.0 + eigen_ref[...])
    w = w.astype(jnp.bfloat16).astype(F32)
    lane = lax.broadcasted_iota(jnp.int32, w.shape, 1)
    ws = []
    for j in range(mode_dev):
        picked = jnp.where(lane == me * mode_dev + j, w, 0.0)
        ws.append(jnp.sum(picked, axis=1, keepdims=True))
    for take in takes[2:]:
        take.wait()
    st_out[0] = bed_ref[...].astype(jnp.bfloat16)
    st_out[1] = smb_ref[...].astype(jnp.bfloat16)
    st_out[2] = h0_ref[...].astype(jnp.bfloat16)

    with jax.named_scope("barrier_w"):
        pl.semaphore_wait(barrier, 4 + B - 1)

    def remote(src, dst, ssem, rsem, peer):
        return pltpu.make_async_remote_copy(
            src_ref=src, dst_ref=dst, send_sem=ssem, recv_sem=rsem,
            device_id={"modes": peer}, device_id_type=pl.DeviceIdType.MESH)

    def halo(kind, side):
        src = (st_out, f_out)[kind]
        dst = (st_in, f_in)[kind]
        peer = right if side == 0 else left
        at = kind * 2 + side
        return remote(src, dst.at[side], hs.at[at], hr.at[at], peer)

    has_up, has_down = me > 0, me < n - 1
    at4 = me % 4

    def send_halo(kind, side, ok):
        here = has_down if side == 0 else has_up

        @pl.when(jnp.logical_and(here, ok))
        def _():
            halo(kind, side).start()

    def wait_halo(kind):
        @pl.when(has_down)
        def _():
            halo(kind, 0).wait_send()
            halo(kind, 1).wait_recv()

        @pl.when(has_up)
        def _():
            halo(kind, 1).wait_send()
            halo(kind, 0).wait_recv()

    send_halo(0, 0, at4 != 1)
    send_halo(0, 1, at4 != 2)

    CT = min(512, cw)

    def col_loop(body, width=cw):
        def step(j, carry):
            body(pl.ds(pl.multiple_of(j * CT, CT), CT))
            return carry
        lax.fori_loop(0, width // CT, step, 0)

    def partial(i, out):
        load(i).wait()

        def body(cs):
            tot = None
            for j in range(mode_dev):
                term = mf[i, j, :, cs].astype(F32) * ws[j]
                tot = term if tot is None else tot + term
            out[:, cs] = tot
        col_loop(body)

    def s1copy(m):
        return remote(p1out.at[m], p1in.at[m], p1s.at[m], p1r.at[m], core_peer)

    def stage1(m):
        with jax.named_scope("s1_%d" % m):
            partial(2 * m, p1out.at[m])
            s1copy(m).start()
            partial(2 * m + 1, p1own.at[m])

    def s2copy(q):
        return remote(s2out.at[q], s2in.at[q], s2s.at[q], s2r.at[q], y_peer)

    def stage2(q):
        with jax.named_scope("s2_%d" % q):
            s1copy(q).wait_recv()

            def body(cs):
                s2out[q, :, cs] = (p1own[q, :, cs] + p1in[q, :, cs]).astype(WIRE)
            col_loop(body)
            s2copy(q).start()

    def s3copy(q):
        return remote(s3out.at[q], s3in.at[q], s3s.at[q], s3r.at[q], z_peer(ks[q // H]))

    def stage3(q):
        with jax.named_scope("s3_%d" % q):
            m = Q + q
            s1copy(m).wait_recv()
            s2copy(q).wait_recv()
            k, hh = ks[q // H], q % H

            def body(cs):
                tot = p1own[m, :, cs] + p1in[m, :, cs] + s2in[q, :, cs].astype(F32)
                if k:
                    s3out[q, :, cs] = tot.astype(WIRE)
                else:
                    p1own[m, :, cs] = tot
            col_loop(body)
            if k:
                s3copy(q).start()

    tiles = cols // LANES
    top, mid, low = pl.ds(PAD, rows), pl.ds(PAD + rows, rows), pl.ds(PAD + 2 * rows, rows)
    whole = 3 * rows + 2 * PAD

    def clear(ref, where, size):
        for j in range(tiles):
            ref[j + 1, where, :] = jnp.zeros((size, LANES), F32)

    def lanes(j):
        return slice(j * LANES, (j + 1) * LANES)

    stage1(0)
    for q in range(1, Q):
        stage1(q)
        stage2(q - 1)
    stage1(Q)
    stage2(Q - 1)
    send_halo(0, 0, at4 == 1)
    send_halo(0, 1, at4 == 2)
    for q in range(1, Q):
        stage1(Q + q)

    clear(ext_s, pl.ds(0, PAD), PAD)
    clear(ext_s, pl.ds(PAD + 3 * rows, PAD), PAD)
    for j in (0, tiles + 1):
        ext_s[j] = jnp.zeros((whole, LANES), F32)
    for j in range(tiles):
        bb, hh = bed_ref[:, lanes(j)], h0_ref[:, lanes(j)]
        ext_b[j + 1, mid, :] = bb
        ext_m[j + 1, mid, :] = time_step * smb_ref[:, lanes(j)]
        ext_h[j + 1, mid, :] = hh
        ext_s[j + 1, mid, :] = bb + hh

    for q in range(Q):
        stage3(q)
    with jax.named_scope("s3wait"):
        for q in range(Q - H):
            s3copy(q).wait_recv()

    def finish(hh):
        off = hh * cw

        def body(cs):
            tot = p1own[2 * Q - H + hh, :, cs]
            for q in range(hh, Q - H, H):
                tot = tot + s3in[q, :, cs].astype(F32)
            return tot

        def step(j, carry):
            cs = pl.ds(pl.multiple_of(j * CT, CT), CT)
            out = pl.ds(pl.multiple_of(off + j * CT, CT), CT)
            tot = body(cs) + map_ref[:, out]
            logf_ref[:, out] = tot
            f_out[:, out] = tot.astype(jnp.bfloat16)
            return carry
        lax.fori_loop(0, cw // CT, step, 0)
    for hh in range(H):
        finish(hh)
    send_halo(1, 0, True)
    send_halo(1, 1, True)

    for j in range(tiles):
        ext_e[j + 1, mid, :] = slide_rate * jnp.exp(-logf_ref[:, lanes(j)])
    with jax.named_scope("halo0"):
        wait_halo(0)

    def fill(side, where, present):
        @pl.when(present)
        def _():
            for j in range(tiles):
                bb = st_in[side, 0, :, lanes(j)].astype(F32)
                hh = st_in[side, 2, :, lanes(j)].astype(F32)
                ext_b[j + 1, where, :] = bb
                ext_m[j + 1, where, :] = time_step * st_in[side, 1, :, lanes(j)].astype(F32)
                ext_h[j + 1, where, :] = hh
                ext_s[j + 1, where, :] = bb + hh

        @pl.when(jnp.logical_not(present))
        def _():
            clear(ext_s, where, rows)
    fill(0, top, has_up)
    fill(1, low, has_down)
    for m in range(2 * Q):
        s1copy(m).wait_send()
    for q in range(Q):
        s2copy(q).wait_send()
        if ks[q // H]:
            s3copy(q).wait_send()
    with jax.named_scope("halo1"):
        wait_halo(1)

    def fill_e(side, where, present):
        @pl.when(present)
        def _():
            for j in range(tiles):
                ext_e[j + 1, where, :] = slide_rate * jnp.exp(-f_in[side, :, lanes(j)].astype(F32))
    fill_e(0, top, has_up)
    fill_e(1, low, has_down)


def step_kernel(n, rows, logf_ref, ext_b, ext_e, ext_m, in_h, in_s, logf_hbm, final_hbm, final_ref, out_sem, ext_h, ext_d, ext_g, ext_s0, ext_s1):
    me = lax.axis_index("modes")
    has_up, has_down = me > 0, me < n - 1
    tiles = ext_b.shape[0] - 2
    whole = 3 * rows + 2 * PAD
    top, mid, low = pl.ds(PAD, rows), pl.ds(PAD + rows, rows), pl.ds(PAD + 2 * rows, rows)
    gives = [pltpu.make_async_copy(x, y, out_sem.at[i]) for i, (x, y) in enumerate(((logf_ref, logf_hbm), (final_ref, final_hbm)))]
    gives[0].start()

    def lanes(j):
        return slice(j * LANES, (j + 1) * LANES)

    def clear(ref, where, size):
        for j in range(tiles):
            ref[j + 1, where, :] = jnp.zeros((size, LANES), F32)

    for ref in (ext_s0, ext_s1, ext_d):
        clear(ref, pl.ds(0, PAD), PAD)
        clear(ref, pl.ds(PAD + 3 * rows, PAD), PAD)
        for j in (0, tiles + 1):
            ref[j] = jnp.zeros((whole, LANES), F32)
    ext_g[0] = jnp.zeros((whole, LANES), F32)
    for where, present in ((top, has_up), (low, has_down)):
        @pl.when(jnp.logical_not(present))
        def _():
            for ref in (ext_s0, ext_s1, ext_d):
                clear(ref, where, rows)

    margin = rows - 2 * STEPS

    def sweep(first, last, body):
        for lo, hi, present in ((0, rows, has_up), (rows, 2 * rows, None), (2 * rows, 3 * rows, has_down)):
            lo, hi = max(lo, first // 8 * 8), min(hi, -(-last // 8) * 8)
            if lo >= hi:
                continue
            if present is None:
                body(PAD + lo, hi - lo)
            else:
                pl.when(present)(functools.partial(body, PAD + lo, hi - lo))

    for t in range(1, STEPS + 1):
        s_ref, s_new = (ext_s0, ext_s1) if t % 2 else (ext_s1, ext_s0)
        s_ref, h_ref = (in_s, in_h) if t == 1 else (s_ref, ext_h)
        lo_h = margin + 2 * t

        lane = lax.broadcasted_iota(jnp.int32, (1, 8, LANES), 2)
        first_lane, last_lane = lane == 0, lane == LANES - 1

        def d_rows(r, size):
            for at in range(r, r + size, 8):
                here, up, down = (slice(at + o, at + o + 8) for o in (0, -1, 1))
                for j in range(1, tiles + 1, GROUP):
                    now, later, sooner = (slice(j + o, j + o + GROUP) for o in (0, 1, -1))
                    s = s_ref[now, here, :]
                    right = pltpu.roll(jnp.where(first_lane, s_ref[later, here, :], s), LANES - 1, 2)
                    left_ = pltpu.roll(jnp.where(last_lane, s_ref[sooner, here, :], s), 1, 2)
                    gx = s_ref[now, down, :] - s_ref[now, up, :]
                    gy = right - left_
                    h = h_ref[now, here, :]
                    sq = h * h
                    d = sq * ((0.25 * flow_rate) * (sq * h) * (gx * gx + gy * gy) + ext_e[now, here, :])
                    ext_d[now, here, :] = jnp.minimum(d, diff_cap)
                    ext_g[now, here, :] = right - s

        def h_rows(r, size):
            for at in range(r, r + size, 8):
                here, up, down = (slice(at + o, at + o + 8) for o in (0, -1, 1))
                edge = pltpu.roll(ext_d[1:2, here, :] * s_ref[1:2, here, :], LANES - 1, 2)
                for j in range(1, tiles + 1, GROUP):
                    now, later = (slice(j + o, j + o + GROUP) for o in (0, 1))
                    s, d = s_ref[now, here, :], ext_d[now, here, :]
                    right = pltpu.roll(jnp.where(first_lane, ext_d[later, here, :], d), LANES - 1, 2)
                    flux = (right + d) * ext_g[now, here, :]
                    sooner = jnp.concatenate([edge, flux[:-1]], axis=0)
                    edge = flux[-1:]
                    div = (ext_d[now, down, :] + d) * (s_ref[now, down, :] - s)
                    div += (ext_d[now, up, :] + d) * (s_ref[now, up, :] - s)
                    div += flux - pltpu.roll(jnp.where(last_lane, sooner, flux), 1, 2)
                    h = jnp.maximum(h_ref[now, here, :] + ((0.5 * time_step) * div + ext_m[now, here, :]), 0.0)
                    ext_h[now, here, :] = h
                    if t < STEPS:
                        s_new[now, here, :] = ext_b[now, here, :] + h

        with jax.named_scope("step%d_d" % t):
            sweep(lo_h - 1, 3 * rows - lo_h + 1, d_rows)
        with jax.named_scope("step%d_h" % t):
            sweep(lo_h, 3 * rows - lo_h, h_rows)

    for j in range(tiles):
        final_ref[:, lanes(j)] = ext_h[j + 1, mid, :]
    gives[1].start()
    gives[0].wait()
    gives[1].wait()


def per_device(n, mode_fields, coeff, eigen, map_friction, bed, smb, thickness):
    rows, cols = map_friction.shape
    mode_dev = mode_fields.shape[0]
    B = n // 4
    H = 2 if n <= 16 else 1
    Q = B * H
    modes = coeff.shape[0]
    anywhere = pl.BlockSpec(memory_space=pl.ANY)
    vmem = pl.BlockSpec(memory_space=pltpu.VMEM)
    strip = (rows, cols)
    part = (rows, cols // H)
    ext = (cols // LANES + 2, 3 * rows + 2 * PAD, LANES)
    bf = jnp.bfloat16
    dma = pltpu.SemaphoreType.DMA
    outs = pl.pallas_call(
        functools.partial(gather_kernel, n, H),
        out_shape=(pltpu.VMEM(strip, F32),) + (pltpu.VMEM(ext, F32),) * 5,
        in_specs=[anywhere] * 7,
        out_specs=(vmem,) * 6,
        scratch_shapes=[
            pltpu.VMEM((1, modes), F32),
            pltpu.VMEM((1, modes), F32),
        ] + [pltpu.VMEM(strip, F32)] * 4 + [
            dma((6,)),
            pltpu.VMEM((n * H, mode_dev) + part, bf),
            pltpu.VMEM((2 * Q,) + part, F32),
            pltpu.VMEM((2 * Q,) + part, F32),
            pltpu.VMEM((2 * Q,) + part, F32),
            pltpu.VMEM((Q,) + part, WIRE),
            pltpu.VMEM((Q,) + part, WIRE),
            pltpu.VMEM((Q,) + part, WIRE),
            pltpu.VMEM((Q,) + part, WIRE),
            pltpu.VMEM((3,) + strip, bf),
            pltpu.VMEM((2, 3) + strip, bf),
            pltpu.VMEM(strip, bf),
            pltpu.VMEM((2,) + strip, bf),
            dma((n * H,)), dma((2 * Q,)), dma((2 * Q,)), dma((Q,)), dma((Q,)), dma((Q,)), dma((Q,)), dma((4,)), dma((4,)),
        ],
        compiler_params=pltpu.CompilerParams(collective_id=0, has_side_effects=True, vmem_limit_bytes=52 * 2**20),
        name="posterior_gather",
    )(coeff.reshape(1, modes), eigen.reshape(1, modes), map_friction, bed, smb, thickness, mode_fields)
    return pl.pallas_call(
        functools.partial(step_kernel, n, rows),
        out_shape=(jax.ShapeDtypeStruct(strip, F32),) * 2,
        in_specs=[vmem] * 6,
        out_specs=(anywhere, anywhere),
        scratch_shapes=[pltpu.VMEM(strip, F32), dma((2,))] + [pltpu.VMEM(ext, F32)] * 5,
        compiler_params=pltpu.CompilerParams(vmem_limit_bytes=16 * 2**20),
        name="ice_steps",
    )(*outs)


def solution(mesh):
    n = mesh.shape["modes"]
    return jax.shard_map(
        functools.partial(per_device, n),
        mesh=mesh,
        in_specs=(
            P(("groups", "modes"), None, None),
            P("groups"),
            P("groups"),
            P(("groups", "modes"), None),
            P(("groups", "modes"), None),
            P(("groups", "modes"), None),
            P(("groups", "modes"), None),
        ),
        out_specs=(P(("groups", "modes"), None), P(("groups", "modes"), None)),
        check_vma=False,
    )
```

```python
import functools

import jax
import jax.numpy as jnp
from jax import lax
from jax.experimental import pallas as pl
from jax.experimental.pallas import tpu as pltpu
from jax.sharding import PartitionSpec as P

STEPS = 8

flow_rate = 0.02
slide_rate = 0.1
diff_cap = 0.5
time_step = 0.4

WIRE = jnp.bfloat16
PAD = 8
LANES = 128
GROUP = 4
F32 = jnp.float32


def flip(x, k):
    bit = 1
    while bit <= k:
        if k & bit:
            x = x + bit - 2 * bit * (x // bit % 2)
        bit *= 2
    return x


def gather_kernel(
    n, H,
    coeff_hbm, eigen_hbm, map_hbm, bed_hbm, smb_hbm, h0_hbm, fields_ref,
    logf_ref, ext_b, ext_e, ext_m, ext_h, ext_s,
    coeff_ref, eigen_ref, map_ref, bed_ref, smb_ref, h0_ref, in_sem,
    mf, p1out, p1own, p1in, s2out, s2in, s3out, s3in,
    st_out, st_in, f_out, f_in,
    mf_sem, p1s, p1r, s2s, s2r, s3s, s3r, hs, hr,
):
    me = lax.axis_index("modes")
    c = me % 2
    a = (me // 2) % 2
    b = me // 4
    B = n // 4
    mode_dev = fields_ref.shape[0]
    rows, cols = map_ref.shape
    cw = cols // H
    ks = list(range(B - 1, -1, -1))
    Q = B * H

    hbm = (coeff_hbm, eigen_hbm, bed_hbm, smb_hbm, h0_hbm, map_hbm)
    own = (coeff_ref, eigen_ref, bed_ref, smb_ref, h0_ref, map_ref)
    takes = [pltpu.make_async_copy(x, y, in_sem.at[i]) for i, (x, y) in enumerate(zip(hbm, own))]
    for take in takes:
        take.start()

    def load(i):
        k, aa, hh, cc = B - 1 - i // (2 * H) % B, 1 - i // (2 * Q), i // 2 % H, 1 - i % 2
        bit, z = 1, b
        while bit < B:
            on = k // bit % 2
            z = z + on * (bit - 2 * bit * (b // bit % 2))
            bit *= 2
        strip = (z * 2 + (a + aa - 2 * a * aa)) * 2 + (c + cc - 2 * c * cc)
        rr = pl.ds(pl.multiple_of(strip * rows, rows), rows)
        cc_ = pl.ds(pl.multiple_of(hh * cw, cw), cw)
        return pltpu.make_async_copy(fields_ref.at[:, rr, cc_], mf.at[i], mf_sem.at[i])

    def go(i, carry):
        load(i).start()
        return carry
    lax.fori_loop(0, n * H, go, 0)

    left, right = lax.rem(me + n - 1, n), lax.rem(me + 1, n)
    core_peer = me + 1 - 2 * c
    y_peer = me + 2 - 4 * a
    barrier = pltpu.get_barrier_semaphore()

    def z_peer(k):
        return (flip(b, k) * 2 + a) * 2 + c

    has_up, has_down = me > 0, me < n - 1

    def greet(peer):
        pl.semaphore_signal(barrier, inc=1, device_id={"modes": peer}, device_id_type=pl.DeviceIdType.MESH)

    for peer in [core_peer, y_peer] + [z_peer(k) for k in range(1, B)]:
        greet(peer)
    pl.when(has_up)(lambda: greet(left))
    pl.when(has_down)(lambda: greet(right))

    takes[0].wait()
    takes[1].wait()
    w = coeff_ref[...] / jnp.sqrt(1.0 + eigen_ref[...])
    w = w.astype(jnp.bfloat16).astype(F32)
    lane = lax.broadcasted_iota(jnp.int32, w.shape, 1)
    ws = []
    for j in range(mode_dev):
        picked = jnp.where(lane == me * mode_dev + j, w, 0.0)
        ws.append(jnp.sum(picked, axis=1, keepdims=True))

    def remote(src, dst, ssem, rsem, peer):
        return pltpu.make_async_remote_copy(
            src_ref=src, dst_ref=dst, send_sem=ssem, recv_sem=rsem,
            device_id={"modes": peer}, device_id_type=pl.DeviceIdType.MESH)

    def halo(kind, side):
        src = (st_out, f_out)[kind]
        dst = (st_in, f_in)[kind]
        peer = right if side == 0 else left
        at = kind * 2 + side
        return remote(src, dst.at[side], hs.at[at], hr.at[at], peer)

    at4 = me % 4

    def send_halo(kind, side, ok):
        here = has_down if side == 0 else has_up

        @pl.when(jnp.logical_and(here, ok))
        def _():
            halo(kind, side).start()

    def wait_halo(kind):
        @pl.when(has_down)
        def _():
            halo(kind, 0).wait_send()
            halo(kind, 1).wait_recv()

        @pl.when(has_up)
        def _():
            halo(kind, 1).wait_send()
            halo(kind, 0).wait_recv()

    CT = min(512, cw)

    def col_loop(body, width=cw):
        def step(j, carry):
            body(pl.ds(pl.multiple_of(j * CT, CT), CT))
            return carry
        lax.fori_loop(0, width // CT, step, 0)

    def partial(i, out):
        load(i).wait()

        def body(cs):
            tot = None
            for j in range(mode_dev):
                term = mf[i, j, :, cs].astype(F32) * ws[j]
                tot = term if tot is None else tot + term
            out[:, cs] = tot
        col_loop(body)

    def s1copy(m):
        return remote(p1out.at[m], p1in.at[m], p1s.at[m], p1r.at[m], core_peer)

    def stage1(m):
        with jax.named_scope("s1_%d" % m):
            partial(2 * m, p1out.at[m])
            s1copy(m).start()
            partial(2 * m + 1, p1own.at[m])

    def meet():
        with jax.named_scope("barrier_w"):
            pl.semaphore_wait(barrier, B + 1 + (me + n - 1) // n + (2 * n - 2 - me) // n)

    def s2copy(q):
        return remote(s2out.at[q], s2in.at[q], s2s.at[q], s2r.at[q], y_peer)

    def stage2(q):
        with jax.named_scope("s2_%d" % q):
            s1copy(q).wait_recv()

            def body(cs):
                s2out[q, :, cs] = (p1own[q, :, cs] + p1in[q, :, cs]).astype(WIRE)
            col_loop(body)
            s2copy(q).start()

    def s3copy(q):
        return remote(s3out.at[q], s3in.at[q], s3s.at[q], s3r.at[q], z_peer(ks[q // H]))

    def stage3(q):
        with jax.named_scope("s3_%d" % q):
            m = Q + q
            s1copy(m).wait_recv()
            s2copy(q).wait_recv()
            k, hh = ks[q // H], q % H

            def body(cs):
                tot = p1own[m, :, cs] + p1in[m, :, cs] + s2in[q, :, cs].astype(F32)
                if k:
                    s3out[q, :, cs] = tot.astype(WIRE)
                else:
                    p1own[m, :, cs] = tot
            col_loop(body)
            if k:
                s3copy(q).start()

    tiles = cols // LANES
    top, mid, low = pl.ds(PAD, rows), pl.ds(PAD + rows, rows), pl.ds(PAD + 2 * rows, rows)
    whole = 3 * rows + 2 * PAD

    def clear(ref, where, size):
        for j in range(tiles):
            ref[j + 1, where, :] = jnp.zeros((size, LANES), F32)

    def lanes(j):
        return slice(j * LANES, (j + 1) * LANES)

    partial(0, p1out.at[0])
    meet()
    s1copy(0).start()
    partial(1, p1own.at[0])
    lead = 4
    for m in range(1, lead):
        stage1(m)
    for take in takes[2:]:
        take.wait()
    st_out[0] = bed_ref[...].astype(jnp.bfloat16)
    st_out[1] = smb_ref[...].astype(jnp.bfloat16)
    st_out[2] = h0_ref[...].astype(jnp.bfloat16)
    send_halo(0, 0, c == 0)
    send_halo(0, 1, c == 1)
    for q in range(Q):
        stage1(q + lead)
        stage2(q)
    send_halo(0, 0, at4 == 1)
    send_halo(0, 1, at4 == 2)
    for m in range(Q + lead, 2 * Q):
        stage1(m)

    clear(ext_s, pl.ds(0, PAD), PAD)
    clear(ext_s, pl.ds(PAD + 3 * rows, PAD), PAD)
    for j in (0, tiles + 1):
        ext_s[j] = jnp.zeros((whole, LANES), F32)
    for j in range(tiles):
        bb, hh = bed_ref[:, lanes(j)], h0_ref[:, lanes(j)]
        ext_b[j + 1, mid, :] = bb
        ext_m[j + 1, mid, :] = time_step * smb_ref[:, lanes(j)]
        ext_h[j + 1, mid, :] = hh
        ext_s[j + 1, mid, :] = bb + hh

    for q in range(Q):
        stage3(q)
    send_halo(0, 0, at4 == 3)
    send_halo(0, 1, at4 == 0)
    with jax.named_scope("s3wait"):
        for q in range(Q - H):
            s3copy(q).wait_recv()

    def finish(hh):
        off = hh * cw

        def body(cs):
            tot = p1own[2 * Q - H + hh, :, cs]
            for q in range(hh, Q - H, H):
                tot = tot + s3in[q, :, cs].astype(F32)
            return tot

        def step(j, carry):
            cs = pl.ds(pl.multiple_of(j * CT, CT), CT)
            out = pl.ds(pl.multiple_of(off + j * CT, CT), CT)
            tot = body(cs) + map_ref[:, out]
            logf_ref[:, out] = tot
            f_out[:, out] = tot.astype(jnp.bfloat16)
            return carry
        lax.fori_loop(0, cw // CT, step, 0)
    for hh in range(H):
        finish(hh)
    send_halo(1, 0, True)
    send_halo(1, 1, True)

    for j in range(tiles):
        ext_e[j + 1, mid, :] = slide_rate * jnp.exp(-logf_ref[:, lanes(j)])
    with jax.named_scope("halo0"):
        wait_halo(0)

    def fill(side, where, present):
        @pl.when(present)
        def _():
            for j in range(tiles):
                bb = st_in[side, 0, :, lanes(j)].astype(F32)
                hh = st_in[side, 2, :, lanes(j)].astype(F32)
                ext_b[j + 1, where, :] = bb
                ext_m[j + 1, where, :] = time_step * st_in[side, 1, :, lanes(j)].astype(F32)
                ext_h[j + 1, where, :] = hh
                ext_s[j + 1, where, :] = bb + hh

        @pl.when(jnp.logical_not(present))
        def _():
            clear(ext_s, where, rows)
    fill(0, top, has_up)
    fill(1, low, has_down)
    for m in range(2 * Q):
        s1copy(m).wait_send()
    for q in range(Q):
        s2copy(q).wait_send()
        if ks[q // H]:
            s3copy(q).wait_send()
    with jax.named_scope("halo1"):
        wait_halo(1)

    def fill_e(side, where, present):
        @pl.when(present)
        def _():
            for j in range(tiles):
                ext_e[j + 1, where, :] = slide_rate * jnp.exp(-f_in[side, :, lanes(j)].astype(F32))
    fill_e(0, top, has_up)
    fill_e(1, low, has_down)


def step_kernel(n, rows, logf_ref, ext_b, ext_e, ext_m, in_h, in_s, logf_hbm, final_hbm, final_ref, out_sem, ext_h, ext_d, ext_g, ext_s0, ext_s1):
    me = lax.axis_index("modes")
    has_up, has_down = me > 0, me < n - 1
    tiles = ext_b.shape[0] - 2
    whole = 3 * rows + 2 * PAD
    top, mid, low = pl.ds(PAD, rows), pl.ds(PAD + rows, rows), pl.ds(PAD + 2 * rows, rows)
    gives = [pltpu.make_async_copy(x, y, out_sem.at[i]) for i, (x, y) in enumerate(((logf_ref, logf_hbm), (final_ref, final_hbm)))]
    gives[0].start()

    def lanes(j):
        return slice(j * LANES, (j + 1) * LANES)

    def clear(ref, where, size):
        for j in range(tiles):
            ref[j + 1, where, :] = jnp.zeros((size, LANES), F32)

    for ref in (ext_s0, ext_s1, ext_d):
        clear(ref, pl.ds(0, PAD), PAD)
        clear(ref, pl.ds(PAD + 3 * rows, PAD), PAD)
        for j in (0, tiles + 1):
            ref[j] = jnp.zeros((whole, LANES), F32)
    ext_g[0] = jnp.zeros((whole, LANES), F32)
    for where, present in ((top, has_up), (low, has_down)):
        @pl.when(jnp.logical_not(present))
        def _():
            for ref in (ext_s0, ext_s1, ext_d):
                clear(ref, where, rows)

    margin = rows - 2 * STEPS

    def sweep(first, last, body):
        for lo, hi, present in ((0, rows, has_up), (rows, 2 * rows, None), (2 * rows, 3 * rows, has_down)):
            lo, hi = max(lo, first // 8 * 8), min(hi, -(-last // 8) * 8)
            if lo >= hi:
                continue
            if present is None:
                body(PAD + lo, hi - lo)
            else:
                pl.when(present)(functools.partial(body, PAD + lo, hi - lo))

    for t in range(1, STEPS + 1):
        s_ref, s_new = (ext_s0, ext_s1) if t % 2 else (ext_s1, ext_s0)
        s_ref, h_ref = (in_s, in_h) if t == 1 else (s_ref, ext_h)
        lo_h = margin + 2 * t

        lane = lax.broadcasted_iota(jnp.int32, (1, 8, LANES), 2)
        first_lane, last_lane = lane == 0, lane == LANES - 1

        def d_rows(r, size):
            for at in range(r, r + size, 8):
                here, up, down = (slice(at + o, at + o + 8) for o in (0, -1, 1))
                for j in range(1, tiles + 1, GROUP):
                    now, later, sooner = (slice(j + o, j + o + GROUP) for o in (0, 1, -1))
                    s = s_ref[now, here, :]
                    right = pltpu.roll(jnp.where(first_lane, s_ref[later, here, :], s), LANES - 1, 2)
                    left_ = pltpu.roll(jnp.where(last_lane, s_ref[sooner, here, :], s), 1, 2)
                    gx = s_ref[now, down, :] - s_ref[now, up, :]
                    gy = right - left_
                    h = h_ref[now, here, :]
                    sq = h * h
                    d = sq * ((0.25 * flow_rate) * (sq * h) * (gx * gx + gy * gy) + ext_e[now, here, :])
                    ext_d[now, here, :] = jnp.minimum(d, diff_cap)
                    ext_g[now, here, :] = right - s

        def h_rows(r, size):
            for at in range(r, r + size, 8):
                here, up, down = (slice(at + o, at + o + 8) for o in (0, -1, 1))
                edge = pltpu.roll(ext_d[1:2, here, :] * s_ref[1:2, here, :], LANES - 1, 2)
                for j in range(1, tiles + 1, GROUP):
                    now, later = (slice(j + o, j + o + GROUP) for o in (0, 1))
                    s, d = s_ref[now, here, :], ext_d[now, here, :]
                    right = pltpu.roll(jnp.where(first_lane, ext_d[later, here, :], d), LANES - 1, 2)
                    flux = (right + d) * ext_g[now, here, :]
                    sooner = jnp.concatenate([edge, flux[:-1]], axis=0)
                    edge = flux[-1:]
                    div = (ext_d[now, down, :] + d) * (s_ref[now, down, :] - s)
                    div += (ext_d[now, up, :] + d) * (s_ref[now, up, :] - s)
                    div += flux - pltpu.roll(jnp.where(last_lane, sooner, flux), 1, 2)
                    h = jnp.maximum(h_ref[now, here, :] + ((0.5 * time_step) * div + ext_m[now, here, :]), 0.0)
                    ext_h[now, here, :] = h
                    if t < STEPS:
                        s_new[now, here, :] = ext_b[now, here, :] + h

        with jax.named_scope("step%d_d" % t):
            sweep(lo_h - 1, 3 * rows - lo_h + 1, d_rows)
        with jax.named_scope("step%d_h" % t):
            sweep(lo_h, 3 * rows - lo_h, h_rows)

    for j in range(tiles):
        final_ref[:, lanes(j)] = ext_h[j + 1, mid, :]
    gives[1].start()
    gives[0].wait()
    gives[1].wait()


def per_device(n, mode_fields, coeff, eigen, map_friction, bed, smb, thickness):
    rows, cols = map_friction.shape
    mode_dev = mode_fields.shape[0]
    B = n // 4
    H = 2 if n <= 16 else 1
    Q = B * H
    modes = coeff.shape[0]
    anywhere = pl.BlockSpec(memory_space=pl.ANY)
    vmem = pl.BlockSpec(memory_space=pltpu.VMEM)
    strip = (rows, cols)
    part = (rows, cols // H)
    ext = (cols // LANES + 2, 3 * rows + 2 * PAD, LANES)
    bf = jnp.bfloat16
    dma = pltpu.SemaphoreType.DMA
    outs = pl.pallas_call(
        functools.partial(gather_kernel, n, H),
        out_shape=(pltpu.VMEM(strip, F32),) + (pltpu.VMEM(ext, F32),) * 5,
        in_specs=[anywhere] * 7,
        out_specs=(vmem,) * 6,
        scratch_shapes=[
            pltpu.VMEM((1, modes), F32),
            pltpu.VMEM((1, modes), F32),
        ] + [pltpu.VMEM(strip, F32)] * 4 + [
            dma((6,)),
            pltpu.VMEM((n * H, mode_dev) + part, bf),
            pltpu.VMEM((2 * Q,) + part, F32),
            pltpu.VMEM((2 * Q,) + part, F32),
            pltpu.VMEM((2 * Q,) + part, F32),
            pltpu.VMEM((Q,) + part, WIRE),
            pltpu.VMEM((Q,) + part, WIRE),
            pltpu.VMEM((Q,) + part, WIRE),
            pltpu.VMEM((Q,) + part, WIRE),
            pltpu.VMEM((3,) + strip, bf),
            pltpu.VMEM((2, 3) + strip, bf),
            pltpu.VMEM(strip, bf),
            pltpu.VMEM((2,) + strip, bf),
            dma((n * H,)), dma((2 * Q,)), dma((2 * Q,)), dma((Q,)), dma((Q,)), dma((Q,)), dma((Q,)), dma((4,)), dma((4,)),
        ],
        compiler_params=pltpu.CompilerParams(collective_id=0, has_side_effects=True, vmem_limit_bytes=52 * 2**20),
        name="posterior_gather",
    )(coeff.reshape(1, modes), eigen.reshape(1, modes), map_friction, bed, smb, thickness, mode_fields)
    return pl.pallas_call(
        functools.partial(step_kernel, n, rows),
        out_shape=(jax.ShapeDtypeStruct(strip, F32),) * 2,
        in_specs=[vmem] * 6,
        out_specs=(anywhere, anywhere),
        scratch_shapes=[pltpu.VMEM(strip, F32), dma((2,))] + [pltpu.VMEM(ext, F32)] * 5,
        compiler_params=pltpu.CompilerParams(vmem_limit_bytes=16 * 2**20),
        name="ice_steps",
    )(*outs)


def solution(mesh):
    n = mesh.shape["modes"]
    return jax.shard_map(
        functools.partial(per_device, n),
        mesh=mesh,
        in_specs=(
            P(("groups", "modes"), None, None),
            P("groups"),
            P("groups"),
            P(("groups", "modes"), None),
            P(("groups", "modes"), None),
            P(("groups", "modes"), None),
            P(("groups", "modes"), None),
        ),
        out_specs=(P(("groups", "modes"), None), P(("groups", "modes"), None)),
        check_vma=False,
    )
```

```python
import functools

import jax
import jax.numpy as jnp
from jax import lax
from jax.experimental import pallas as pl
from jax.experimental.pallas import tpu as pltpu
from jax.sharding import PartitionSpec as P

STEPS = 8

flow_rate = 0.02
slide_rate = 0.1
diff_cap = 0.5
time_step = 0.4

WIRE = jnp.bfloat16
PAD = 8
LANES = 128
F32 = jnp.float32
SUB = 8

damp = 0.5 * time_step
unit = (damp * 0.25 * flow_rate) ** (1.0 / 7.0)
slide = damp * slide_rate / unit**2
dry = -1e30


def flip(x, k):
    bit = 1
    while bit <= k:
        if k & bit:
            x = x + bit - 2 * bit * (x // bit % 2)
        bit *= 2
    return x


def gather_kernel(
    n, H,
    coeff_hbm, eigen_hbm, map_hbm, bed_hbm, smb_hbm, h0_hbm, fields_ref,
    logf_ref, pl_b, pl_e, pl_m, pl_h,
    coeff_ref, eigen_ref, map_ref, bed_ref, smb_ref, h0_ref, in_sem,
    mf, p1out, p1own, p1in, s2out, s2in, s3out, s3in,
    st_out, st_in, st_via, f_out, f_in, ext_b, ext_e, ext_m, ext_h,
    mf_sem, p1s, p1r, s2s, s2r, s3s, s3r, hs, hr, via_s, via_r,
):
    me = lax.axis_index("modes")
    c = me % 2
    a = (me // 2) % 2
    b = me // 4
    B = n // 4
    mode_dev = fields_ref.shape[0]
    rows, cols = map_ref.shape
    cw = cols // H
    ks = list(range(B - 1, -1, -1))
    Q = B * H

    hbm = (coeff_hbm, eigen_hbm, bed_hbm, smb_hbm, h0_hbm, map_hbm)
    own = (coeff_ref, eigen_ref, bed_ref, smb_ref, h0_ref, map_ref)
    takes = [pltpu.make_async_copy(x, y, in_sem.at[i]) for i, (x, y) in enumerate(zip(hbm, own))]
    for take in takes:
        take.start()

    def load(i):
        k, aa, hh, cc = B - 1 - i // (2 * H) % B, 1 - i // (2 * Q), i // 2 % H, 1 - i % 2
        bit, z = 1, b
        while bit < B:
            on = k // bit % 2
            z = z + on * (bit - 2 * bit * (b // bit % 2))
            bit *= 2
        strip = (z * 2 + (a + aa - 2 * a * aa)) * 2 + (c + cc - 2 * c * cc)
        rr = pl.ds(pl.multiple_of(strip * rows, rows), rows)
        cc_ = pl.ds(pl.multiple_of(hh * cw, cw), cw)
        return pltpu.make_async_copy(fields_ref.at[:, rr, cc_], mf.at[i], mf_sem.at[i])

    def go(i, carry):
        load(i).start()
        return carry
    lax.fori_loop(0, n * H, go, 0)

    left, right = lax.rem(me + n - 1, n), lax.rem(me + 1, n)
    core_peer = me + 1 - 2 * c
    y_peer = me + 2 - 4 * a
    barrier = pltpu.get_barrier_semaphore()

    def z_peer(k):
        return (flip(b, k) * 2 + a) * 2 + c

    has_up, has_down = me > 0, me < n - 1
    at4 = me % 4

    def greet(peer):
        pl.semaphore_signal(barrier, inc=1, device_id={"modes": peer}, device_id_type=pl.DeviceIdType.MESH)

    for peer in [core_peer, y_peer] + [z_peer(k) for k in range(1, B)]:
        greet(peer)
    pl.when(has_up)(lambda: greet(left))
    pl.when(has_down)(lambda: greet(right))
    pl.when(at4 == 0)(lambda: greet(me + 3))
    pl.when(at4 == 3)(lambda: greet(me - 3))

    takes[0].wait()
    takes[1].wait()
    w = coeff_ref[...] / jnp.sqrt(1.0 + eigen_ref[...])
    w = w.astype(jnp.bfloat16).astype(F32)
    lane = lax.broadcasted_iota(jnp.int32, w.shape, 1)
    ws = []
    for j in range(mode_dev):
        picked = jnp.where(lane == me * mode_dev + j, w, 0.0)
        ws.append(jnp.sum(picked, axis=1, keepdims=True))

    def remote(src, dst, ssem, rsem, peer):
        return pltpu.make_async_remote_copy(
            src_ref=src, dst_ref=dst, send_sem=ssem, recv_sem=rsem,
            device_id={"modes": peer}, device_id_type=pl.DeviceIdType.MESH)

    def halo(side):
        return remote(st_out, st_in.at[side], hs.at[side], hr.at[side], right if side == 0 else left)

    def f_halo(hh, side):
        at = 2 + hh * 2 + side
        return remote(f_out.at[hh], f_in.at[side, hh], hs.at[at], hr.at[at], right if side == 0 else left)

    def send_halo(side, ok):
        here = has_down if side == 0 else has_up

        @pl.when(jnp.logical_and(here, ok))
        def _():
            halo(side).start()

    def hop(side):
        return remote(st_out, st_via, hs.at[side], via_r.at[0], me + 4 - 8 * side)

    def forward(side):
        return remote(st_via, st_in.at[side], via_s.at[0], hr.at[side], me - 3 + 6 * side)

    lower, upper = me >= 4, me < n - 4
    seats = [jnp.logical_and(at4 == 3, upper), jnp.logical_and(at4 == 0, lower)]
    vias = [jnp.logical_and(at4 == 3, lower), jnp.logical_and(at4 == 0, upper)]

    def swap(do):
        for side in (0, 1):
            for ok, what in zip((seats[side], vias[side]), do):
                if what:
                    pl.when(ok)(functools.partial(what, side))

    def wait_halo():
        @pl.when(has_down)
        def _():
            halo(0).wait_send()
            halo(1).wait_recv()

        @pl.when(has_up)
        def _():
            halo(1).wait_send()
            halo(0).wait_recv()

    def wait_f():
        for hh in range(H):
            @pl.when(has_down)
            def _():
                f_halo(hh, 0).wait_send()
                f_halo(hh, 1).wait_recv()

            @pl.when(has_up)
            def _():
                f_halo(hh, 1).wait_send()
                f_halo(hh, 0).wait_recv()

    CT = min(512, cw)

    def col_loop(body, width=cw):
        def step(j, carry):
            body(pl.ds(pl.multiple_of(j * CT, CT), CT))
            return carry
        lax.fori_loop(0, width // CT, step, 0)

    def partial(i, out):
        load(i).wait()

        def body(cs):
            tot = None
            for j in range(mode_dev):
                term = mf[i, j, :, cs].astype(F32) * ws[j]
                tot = term if tot is None else tot + term
            out[:, cs] = tot
        col_loop(body)

    def s1copy(m):
        return remote(p1out.at[m], p1in.at[m], p1s.at[m], p1r.at[m], core_peer)

    def stage1(m):
        with jax.named_scope("s1_%d" % m):
            partial(2 * m, p1out.at[m])
            s1copy(m).start()
            partial(2 * m + 1, p1own.at[m])

    def meet():
        with jax.named_scope("barrier_w"):
            pl.semaphore_wait(barrier, B + 1 + (me + n - 1) // n + (2 * n - 2 - me) // n + 1 - (at4 + 1) // 2 % 2)

    def s2copy(q):
        return remote(s2out.at[q], s2in.at[q], s2s.at[q], s2r.at[q], y_peer)

    def stage2(q):
        with jax.named_scope("s2_%d" % q):
            s1copy(q).wait_recv()

            def body(cs):
                s2out[q, :, cs] = (p1own[q, :, cs] + p1in[q, :, cs]).astype(WIRE)
            col_loop(body)
            s2copy(q).start()

    def s3copy(q):
        return remote(s3out.at[q], s3in.at[q], s3s.at[q], s3r.at[q], z_peer(ks[q // H]))

    def stage3(q):
        with jax.named_scope("s3_%d" % q):
            m = Q + q
            s1copy(m).wait_recv()
            s2copy(q).wait_recv()
            k, hh = ks[q // H], q % H

            def body(cs):
                tot = p1own[m, :, cs] + p1in[m, :, cs] + s2in[q, :, cs].astype(F32)
                if k:
                    s3out[q, :, cs] = tot.astype(WIRE)
                else:
                    p1own[m, :, cs] = tot
            col_loop(body)
            if k:
                s3copy(q).start()

    tiles = cols // LANES
    top, mid, low = pl.ds(0, rows), pl.ds(rows, rows), pl.ds(2 * rows, rows)

    def lanes(j):
        return slice(j * LANES, (j + 1) * LANES)

    def turn(ext, planes):
        G = planes.shape[0]
        for g in range(G):
            block = jnp.concatenate([ext[j, pl.ds(g, SUB, stride=G), :] for j in range(tiles)], axis=0)
            planes[g] = block.T

    partial(0, p1out.at[0])
    meet()
    s1copy(0).start()
    partial(1, p1own.at[0])
    lead = 4
    for m in range(1, lead):
        stage1(m)
    for take in takes[2:]:
        take.wait()
    st_out[0] = bed_ref[...].astype(jnp.bfloat16)
    st_out[1] = smb_ref[...].astype(jnp.bfloat16)
    st_out[2] = h0_ref[...].astype(jnp.bfloat16)
    send_halo(0, c == 0)
    send_halo(1, c == 1)
    swap((lambda side: hop(side).start(), None))
    for q in range(Q):
        stage1(q + lead)
        stage2(q)
    send_halo(0, at4 == 1)
    send_halo(1, at4 == 2)
    for m in range(Q + lead, 2 * Q):
        stage1(m)

    for j in range(tiles):
        ext_b[j, mid, :] = unit * bed_ref[:, lanes(j)]
        ext_m[j, mid, :] = (unit * time_step) * smb_ref[:, lanes(j)]
        ext_h[j, mid, :] = unit * h0_ref[:, lanes(j)]

    def pass_on(side):
        hop(side).wait_recv()
        forward(side).start()

    for q in range(Q):
        stage3(q)
        if q == min(1, Q - 1):
            with jax.named_scope("relay"):
                swap((None, pass_on))

    def finish(hh):
        off = hh * cw

        def body(cs):
            tot = p1own[2 * Q - H + hh, :, cs]
            for q in range(hh, Q - H, H):
                tot = tot + s3in[q, :, cs].astype(F32)
            return tot

        def step(j, carry):
            cs = pl.ds(pl.multiple_of(j * CT, CT), CT)
            out = pl.ds(pl.multiple_of(off + j * CT, CT), CT)
            tot = body(cs) + map_ref[:, out]
            logf_ref[:, out] = tot
            f_out[hh, :, cs] = tot.astype(jnp.bfloat16)
            return carry
        lax.fori_loop(0, cw // CT, step, 0)
    for hh in range(H):
        with jax.named_scope("s3wait%d" % hh):
            for q in range(hh, Q - H, H):
                s3copy(q).wait_recv()
        finish(hh)

        @pl.when(has_down)
        def _():
            f_halo(hh, 0).start()

        @pl.when(has_up)
        def _():
            f_halo(hh, 1).start()

    for j in range(tiles):
        ext_e[j, mid, :] = slide * jnp.exp(-logf_ref[:, lanes(j)])
    with jax.named_scope("halo0"):
        wait_halo()

    def fill(side, where, present):
        @pl.when(present)
        def _():
            for j in range(tiles):
                ext_b[j, where, :] = unit * st_in[side, 0, :, lanes(j)].astype(F32)
                ext_m[j, where, :] = (unit * time_step) * st_in[side, 1, :, lanes(j)].astype(F32)
                ext_h[j, where, :] = unit * st_in[side, 2, :, lanes(j)].astype(F32)

        @pl.when(jnp.logical_not(present))
        def _():
            for j in range(tiles):
                ext_b[j, where, :] = jnp.zeros((rows, LANES), F32)
                ext_m[j, where, :] = jnp.full((rows, LANES), dry, F32)
                ext_h[j, where, :] = jnp.zeros((rows, LANES), F32)
    fill(0, top, has_up)
    fill(1, low, has_down)
    with jax.named_scope("turn3"):
        turn(ext_b, pl_b)
        turn(ext_m, pl_m)
        turn(ext_h, pl_h)
    swap((None, lambda side: forward(side).wait_send()))
    for m in range(2 * Q):
        s1copy(m).wait_send()
    for q in range(Q):
        s2copy(q).wait_send()
        if ks[q // H]:
            s3copy(q).wait_send()
    with jax.named_scope("halo1"):
        wait_f()

    def fill_e(side, where, present):
        @pl.when(present)
        def _():
            for j in range(tiles):
                ext_e[j, where, :] = slide * jnp.exp(-f_in[side, j * LANES // cw, :, lanes(j % (cw // LANES))].astype(F32))

        @pl.when(jnp.logical_not(present))
        def _():
            for j in range(tiles):
                ext_e[j, where, :] = jnp.zeros((rows, LANES), F32)
    fill_e(0, top, has_up)
    fill_e(1, low, has_down)
    with jax.named_scope("turn_e"):
        turn(ext_e, pl_e)


def step_kernel(logf_ref, b_ref, e_ref, m_ref, h0_ref, logf_hbm, final_hbm, final_ref, out_sem, h_ref, a_ref, f_ref, d_ref, s0_ref, s1_ref, fin):
    rows, cols = final_ref.shape
    G, span = h_ref.shape[0], h_ref.shape[1]
    tiles = cols // LANES
    gives = [pltpu.make_async_copy(x, y, out_sem.at[i]) for i, (x, y) in enumerate(((logf_ref, logf_hbm), (final_ref, final_hbm)))]
    gives[0].start()

    lane = lax.broadcasted_iota(jnp.int32, (1, LANES), 1)
    inner, outer = lane >= SUB, lane < LANES - SUB

    def before(row):
        return jnp.where(inner, pltpu.roll(row, SUB, 1), 0.0)

    def after(row):
        return jnp.where(outer, pltpu.roll(row, LANES - SUB, 1), 0.0)

    def row(ref, g, i):
        return ref[g, PAD + i:PAD + i + 1, :]

    def at(i):
        return slice(PAD + i, PAD + i + SUB)

    def put(ref, g, i, x):
        ref[g + 1, at(i), :] = x
        if g == G - 1:
            ref[0, at(i), :] = pltpu.roll(x, 1, 1)
        if g == 0:
            ref[G + 1, at(i), :] = pltpu.roll(x, LANES - 1, 1)

    def wrap(ref, g):
        ref[g + 1, PAD - 1:PAD, :] = before(row(ref, g + 1, span - 1))
        ref[g + 1, PAD + span:PAD + span + 1, :] = after(row(ref, g + 1, 0))

    for i in range(0, span, SUB):
        for g in range(G):
            h = h0_ref[g, i:i + SUB, :]
            h_ref[g, i:i + SUB, :] = h
            put(s0_ref, g, i, b_ref[g, i:i + SUB, :] + h)
    for g in range(G):
        wrap(s0_ref, g)

    def step(s_ref, s_new):
        for i in range(0, span, SUB):
            here = slice(i, i + SUB)
            up, s = s_ref[0, at(i), :], s_ref[1, at(i), :]
            for g in range(G):
                down = s_ref[g + 2, at(i), :]
                right = s_ref[g + 1, at(i + 1), :]
                gx = down - up
                gy = right - s_ref[g + 1, at(i - 1), :]
                h = h_ref[g, here, :]
                sq = h * h
                d = sq * ((sq * h) * (gx * gx + gy * gy) + e_ref[g, here, :])
                put(d_ref, g, i, jnp.minimum(d, damp * diff_cap))
                a_ref[g, here, :] = right - s
                up, s = s, down
        for g in range(G):
            wrap(d_ref, g)
            first = row(d_ref, g + 1, 0) + row(d_ref, g + 1, -1)
            f_ref[g, PAD - 1:PAD, :] = first * (row(s_ref, g + 1, 0) - row(s_ref, g + 1, -1))
        for i in range(0, span, SUB):
            here = slice(i, i + SUB)
            fluxes = []
            for g in range(G):
                flux = (d_ref[g + 1, at(i + 1), :] + d_ref[g + 1, at(i), :]) * a_ref[g, here, :]
                f_ref[g, at(i), :] = flux
                fluxes.append(flux)
            s, d = s_ref[1, at(i), :], d_ref[1, at(i), :]
            came = (d + d_ref[0, at(i), :]) * (s - s_ref[0, at(i), :])
            for g in range(G):
                s_down, d_down = s_ref[g + 2, at(i), :], d_ref[g + 2, at(i), :]
                goes = (d_down + d) * (s_down - s)
                div = (goes - came) + (fluxes[g] - f_ref[g, at(i - 1), :])
                h = jnp.maximum((h_ref[g, here, :] + m_ref[g, here, :]) + div, 0.0)
                h_ref[g, here, :] = h
                put(s_new, g, i, b_ref[g, here, :] + h)
                came, s, d = goes, s_down, d_down
        for g in range(G):
            wrap(s_new, g)

    def pair(t, carry):
        with jax.named_scope("pair"):
            step(s0_ref, s1_ref)
            step(s1_ref, s0_ref)
        return carry
    lax.fori_loop(0, STEPS // 2, pair, 0)

    with jax.named_scope("back"):
        for g in range(G):
            block = (h_ref[g] * (1.0 / unit)).T
            for j in range(tiles):
                fin[j, pl.ds(g, SUB, stride=G), :] = block[j * SUB:(j + 1) * SUB]
        for j in range(tiles):
            final_ref[:, j * LANES:(j + 1) * LANES] = fin[j, rows:2 * rows, :]
    gives[1].start()
    gives[0].wait()
    gives[1].wait()


def per_device(n, mode_fields, coeff, eigen, map_friction, bed, smb, thickness):
    rows, cols = map_friction.shape
    mode_dev = mode_fields.shape[0]
    B = n // 4
    H = 2 if n <= 16 else 1
    Q = B * H
    modes = coeff.shape[0]
    anywhere = pl.BlockSpec(memory_space=pl.ANY)
    vmem = pl.BlockSpec(memory_space=pltpu.VMEM)
    strip = (rows, cols)
    part = (rows, cols // H)
    tiles = cols // LANES
    G = 3 * rows // SUB
    ext = (tiles, 3 * rows, LANES)
    planes = (G, LANES, LANES)
    padded = (G + 2, LANES + 2 * PAD, LANES)
    assert tiles * SUB == LANES and G * SUB == 3 * rows and STEPS % 2 == 0
    bf = jnp.bfloat16
    dma = pltpu.SemaphoreType.DMA
    outs = pl.pallas_call(
        functools.partial(gather_kernel, n, H),
        out_shape=(pltpu.VMEM(strip, F32),) + (pltpu.VMEM(planes, F32),) * 4,
        in_specs=[pl.BlockSpec(memory_space=pl.ANY)] * 7,
        out_specs=(vmem,) * 5,
        scratch_shapes=[
            pltpu.VMEM((1, modes), F32),
            pltpu.VMEM((1, modes), F32),
        ] + [pltpu.VMEM(strip, F32)] * 4 + [
            dma((6,)),
            pltpu.VMEM((n * H, mode_dev) + part, bf),
            pltpu.VMEM((2 * Q,) + part, F32),
            pltpu.VMEM((2 * Q,) + part, F32),
            pltpu.VMEM((2 * Q,) + part, F32),
            pltpu.VMEM((Q,) + part, WIRE),
            pltpu.VMEM((Q,) + part, WIRE),
            pltpu.VMEM((Q,) + part, WIRE),
            pltpu.VMEM((Q,) + part, WIRE),
            pltpu.VMEM((3,) + strip, bf),
            pltpu.VMEM((2, 3) + strip, bf),
            pltpu.VMEM((3,) + strip, bf),
            pltpu.VMEM((H,) + part, bf),
            pltpu.VMEM((2, H) + part, bf),
        ] + [pltpu.VMEM(ext, F32)] * 4 + [
            dma((n * H,)), dma((2 * Q,)), dma((2 * Q,)), dma((Q,)), dma((Q,)), dma((Q,)), dma((Q,)), dma((2 + 2 * H,)), dma((2 + 2 * H,)), dma((1,)), dma((1,)),
        ],
        compiler_params=pltpu.CompilerParams(collective_id=0, has_side_effects=True, vmem_limit_bytes=58 * 2**20),
        name="posterior_gather",
    )(coeff.reshape(1, modes), eigen.reshape(1, modes), map_friction, bed, smb, thickness, mode_fields)
    return pl.pallas_call(
        step_kernel,
        out_shape=(jax.ShapeDtypeStruct(strip, F32),) * 2,
        in_specs=[vmem] * 5,
        out_specs=(anywhere, anywhere),
        scratch_shapes=[pltpu.VMEM(strip, F32), dma((2,))] + [pltpu.VMEM(planes, F32)] * 2 + [pltpu.VMEM((G, LANES + 2 * PAD, LANES), F32)]
        + [pltpu.VMEM(padded, F32)] * 3 + [pltpu.VMEM(ext, F32)],
        compiler_params=pltpu.CompilerParams(vmem_limit_bytes=16 * 2**20),
        name="ice_steps",
    )(*outs)


def solution(mesh):
    n = mesh.shape["modes"]
    return jax.shard_map(
        functools.partial(per_device, n),
        mesh=mesh,
        in_specs=(
            P(("groups", "modes"), None, None),
            P("groups"),
            P("groups"),
            P(("groups", "modes"), None),
            P(("groups", "modes"), None),
            P(("groups", "modes"), None),
            P(("groups", "modes"), None),
        ),
        out_specs=(P(("groups", "modes"), None), P(("groups", "modes"), None)),
        check_vma=False,
    )
```
